1024 devices in a mesh: head: 64 (over z, y_hi), ctx: 16 (over x, y_lo, core).
Axes of the slice: x: 4, y: 4 (y_hi: 2, y_lo: 2; y = y_hi * 2 + y_lo), z: 32, core: 2. Of those that a mesh axis runs over, the one named last changes fastest.
Arguments:
- latent: bfloat16 [16, 128, 512], P('ctx', 'head'), may hold values from -6 to 6
- gain: float32 [512], replicated, may hold values from 0.1 to 1.9
- cotangent: bfloat16 [16, 128, 64, 256], P('ctx', None, 'head'), may hold values from -1 to 1
- weight: bfloat16 [512, 64, 256], P('ctx', 'head'), may hold values from -0.25 to 0.25
Outputs:
- latent_gradient: float32 [16, 128, 512], P('ctx', 'head')
- weight_grad: float32 [512, 64, 256], P('ctx', 'head')
The draws below stay inside these ranges and needn't reach their ends.
All inputs are finite; a program needn't handle non-finite values.
Results may differ from the reference program's by a relative error of at most 0.0029.
Values may be sent and summed in bfloat16 or wider, within the bound.
A program may use at most 32 MiB of HBM per device.

```python
import jax
import jax.numpy as jnp
from jax import lax

HEADS = 64
LATENT = 512
KV = 256
CTX_TOK = 128
SHARDS = 16


def spiked(values, key, source, target, parts, factor):
    def block_of(dim):
        return (jnp.arange(values.shape[dim]) // (values.shape[dim] // parts)).reshape((-1,) + (1,) * (values.ndim - 1 - dim))

    first = jax.random.permutation(key, parts)[block_of(target)]
    far = (block_of(target) + parts // 2) % parts
    return jnp.where((block_of(source) == first) | (block_of(source) == far), factor * values, values)


def shard_levels(key, extent, cuts, low, high):
    def one(axis_at, parts):
        steps = jax.random.uniform(jax.random.fold_in(jax.random.fold_in(key, 6), axis_at), (parts,), jnp.float32, low / len(cuts), high / len(cuts))
        return jnp.repeat(jnp.exp(steps), extent[axis_at] // parts).reshape((-1,) + (1,) * (len(extent) - axis_at - 1))

    loudness = one(*cuts[0])
    for cut in cuts[1:]:
        loudness = loudness * one(*cut)
    return loudness


def gaussian(rng, shape, deviation, most, cuts=(), held_as=jnp.bfloat16):
    factor_of = shard_levels(rng, shape, cuts, -0.22, 0.18) if cuts else 1.0
    array = jax.random.normal(rng, shape, jnp.float32) * deviation * factor_of
    return jnp.minimum(jnp.maximum(array, -most), most).astype(held_as)


def bell_draw_with(own_key, extent, spread, bound, cuts, heavy, kind=jnp.bfloat16):
    result = spread * jax.random.normal(own_key, extent, jnp.float32)
    if cuts:
        result = result * shard_levels(own_key, extent, cuts, -0.22, 0.18)
    return jnp.clip(spiked(result, jax.random.fold_in(own_key, 3), *heavy), -bound, bound).astype(kind)


def setup_inputs(seed: int = 0) -> dict:
    seeds = jax.random.split(jax.random.key(seed), 5)
    latent = gaussian(seeds[0], (SHARDS, CTX_TOK, LATENT), 1.0, 6.0, ((0, 16), (1, 64)))
    gain = jnp.clip(1.0 + 0.18 * jax.random.normal(seeds[1], (LATENT,), jnp.float32), 0.1, 1.9)
    cotangent = bell_draw_with(seeds[2], (SHARDS, CTX_TOK, HEADS, KV), 0.125, 1.0, ((0, 16), (2, 64)), (2, 1, 64, 4.0))
    weight = gaussian(seeds[3], (LATENT, HEADS, KV), LATENT ** -0.5, 0.25, ((0, 16), (1, 64)))
    return dict(latent=latent, gain=gain, cotangent=cotangent, weight=weight)


def reference(latent, gain, cotangent, weight):
    raw_latent = latent.astype(jnp.float32).reshape(-1, LATENT)
    root_mean_square = lax.rsqrt(lax.optimization_barrier(jnp.mean(raw_latent * raw_latent, axis=1, keepdims=True)) + 1e-06)
    latent_hat = raw_latent * root_mean_square
    normed_latent = (latent_hat * gain).astype(jnp.bfloat16)
    flat = cotangent.reshape(-1, HEADS * KV)
    weight_flat = weight.reshape(LATENT, HEADS * KV)
    grad_normed = lax.dot_general(flat, weight_flat, (((1,), (1,)), ((), ())), preferred_element_type=jnp.float32)
    weight_grad = lax.dot_general(normed_latent, flat, (((0,), (0,)), ((), ())), preferred_element_type=jnp.float32)
    scaled_latent = grad_normed * gain
    inner_product = lax.optimization_barrier(jnp.mean(scaled_latent * latent_hat, axis=1, keepdims=True))
    latent_gradient = root_mean_square * (scaled_latent - latent_hat * inner_product)
    return (latent_gradient.reshape(latent.shape), weight_grad.reshape(LATENT, HEADS, KV))
```

```python
import functools

import jax
import jax.numpy as jnp
from jax import lax
from jax.experimental import pallas as pl
from jax.experimental.pallas import tpu as pltpu
from jax.sharding import PartitionSpec as P

MESH = pl.DeviceIdType.MESH
F32, BF16 = jnp.float32, jnp.bfloat16


def drain(ref, sem):
    pltpu.make_async_copy(ref, ref, sem).wait()


def kernel(
    heads,
    shards,
    lat_ref,
    gain_ref,
    cot_ref,
    w_ref,
    lg_ref,
    wg_ref,
    own_n,
    n_buf,
    n_mat,
    w_buf,
    g_send,
    g_recv,
    wg_send,
    wg_recv,
    send_sems,
    recv_sems,
):
    h = lax.axis_index("head")
    s = lax.axis_index("ctx")
    owned = lat_ref.shape[0]
    width = lat_ref.shape[1]

    barrier = pltpu.get_barrier_semaphore()

    def greet(axis, count, me):
        def body(i, carry):
            pl.semaphore_signal(
                barrier, 1, device_id={axis: lax.rem(me + i, count)}, device_id_type=MESH
            )
            return carry

        lax.fori_loop(1, count, body, 0)

    greet("head", heads, h)
    greet("ctx", shards, s)

    raw = lat_ref[...].astype(F32)
    rms = lax.rsqrt(jnp.mean(raw * raw, axis=1, keepdims=True) + 1e-06)
    hat = raw * rms
    gain = gain_ref[...]
    own_n[...] = (hat * gain).astype(BF16)
    n_buf[h] = own_n[...]
    w_buf[s] = w_ref[...]

    pl.semaphore_wait(barrier, heads + shards - 2)

    def send(axis, count, me, src, dst, lane):
        def body(i, carry):
            q = lax.rem(me + count // 2 + i, count)

            @pl.when(q != me)
            def _():
                pltpu.make_async_remote_copy(
                    src_ref=src(q),
                    dst_ref=dst,
                    send_sem=send_sems.at[lane],
                    recv_sem=recv_sems.at[lane],
                    device_id={axis: q},
                    device_id_type=MESH,
                ).start()

            return carry

        lax.fori_loop(0, count, body, 0)

    send("ctx", shards, s, lambda q: w_ref, w_buf.at[s], 0)
    send("head", heads, h, lambda q: own_n, n_buf.at[h], 1)

    drain(w_buf.at[pl.ds(0, shards - 1)], recv_sems.at[0])
    whole = w_buf[...].reshape(width, -1)
    g = lax.dot_general(
        cot_ref[...], whole, (((1,), (1,)), ((), ())), preferred_element_type=F32
    ).astype(BF16)
    for q in range(heads):
        g_send[q] = g[owned * q : owned * (q + 1), :]
    g_recv[h] = g_send[h]
    send("head", heads, h, lambda q: g_send.at[q], g_recv.at[h], 2)

    drain(n_buf.at[pl.ds(0, heads - 1)], recv_sems.at[1])
    for q in range(heads):
        n_mat[owned * q : owned * (q + 1), :] = n_buf[q]
    wg = lax.dot_general(
        n_mat[...], cot_ref[...], (((0,), (0,)), ((), ())), preferred_element_type=F32
    )
    wg_send[...] = wg.astype(BF16).reshape(wg_send.shape)
    wg_recv[s] = wg_send[s]
    send("ctx", shards, s, lambda q: wg_send.at[q], wg_recv.at[s], 3)

    drain(g_recv.at[pl.ds(0, heads - 1)], recv_sems.at[2])
    rows = jnp.sum(g_recv[...].astype(F32), axis=0)
    scaled = rows * gain
    inner = jnp.mean(scaled * hat, axis=1, keepdims=True)
    lg_ref[...] = rms * (scaled - hat * inner)

    drain(wg_recv.at[pl.ds(0, shards - 1)], recv_sems.at[3])
    wg_ref[...] = jnp.sum(wg_recv[...].astype(F32), axis=0)

    drain(w_buf.at[pl.ds(0, shards - 1)], send_sems.at[0])
    drain(n_buf.at[pl.ds(0, heads - 1)], send_sems.at[1])
    drain(g_send.at[pl.ds(0, heads - 1)], send_sems.at[2])
    drain(wg_send.at[pl.ds(0, shards - 1)], send_sems.at[3])


def solution(mesh):
    heads, shards = mesh.shape["head"], mesh.shape["ctx"]

    def per_device(latent, gain, cotangent, weight):
        _, owned, width = latent.shape
        tokens, channels = cotangent.shape[1], cotangent.shape[3]
        rows = weight.shape[0]
        vmem = pl.BlockSpec(memory_space=pltpu.VMEM)
        lg, wg = pl.pallas_call(
            functools.partial(kernel, heads, shards),
            out_shape=(
                jax.ShapeDtypeStruct((owned, width), F32),
                jax.ShapeDtypeStruct((rows, channels), F32),
            ),
            in_specs=[vmem] * 4,
            out_specs=(vmem, vmem),
            scratch_shapes=[
                pltpu.VMEM((owned, width), BF16),
                pltpu.VMEM((heads, owned, width), BF16),
                pltpu.VMEM((tokens, width), BF16),
                pltpu.VMEM((shards, rows, channels), BF16),
                pltpu.VMEM((heads, owned, width), BF16),
                pltpu.VMEM((heads, owned, width), BF16),
                pltpu.VMEM((shards, rows, channels), BF16),
                pltpu.VMEM((shards, rows, channels), BF16),
                pltpu.SemaphoreType.DMA((4,)),
                pltpu.SemaphoreType.DMA((4,)),
            ],
            compiler_params=pltpu.CompilerParams(collective_id=0, has_side_effects=True),
            name="fused",
        )(
            latent.reshape(owned, width),
            gain.reshape(1, width),
            cotangent.reshape(tokens, channels),
            weight.reshape(rows, channels),
        )
        return lg.reshape(latent.shape), wg.reshape(weight.shape)

    return jax.shard_map(
        per_device,
        mesh=mesh,
        in_specs=(
            P("ctx", "head", None),
            P(),
            P("ctx", None, "head", None),
            P("ctx", "head", None),
        ),
        out_specs=(P("ctx", "head", None), P("ctx", "head", None)),
        check_vma=False,
    )
```

```python
import functools

import jax
import jax.numpy as jnp
from jax import lax
from jax.experimental import pallas as pl
from jax.experimental.pallas import tpu as pltpu
from jax.sharding import PartitionSpec as P

MESH = pl.DeviceIdType.MESH
F32, BF16 = jnp.float32, jnp.bfloat16
LATE = (28, 54)
REACH = 17
GROUP = 4


def drain(ref, sem):
    pltpu.make_async_copy(ref, ref, sem).wait()


def kernel(
    heads,
    shards,
    lat_hbm,
    gain_hbm,
    cot_hbm,
    w_hbm,
    lg_ref,
    wg_ref,
    lat_ref,
    gain_ref,
    cot_ref,
    own_n,
    n_buf,
    n_mat,
    w_buf,
    g_send,
    g_recv,
    wg_send,
    wg_recv,
    load_sems,
    send_sems,
    recv_sems,
    ctx_go,
    far_go,
    near_go,
):
    h = lax.axis_index("head")
    s = lax.axis_index("ctx")
    core = lax.rem(s, 2)
    partner = s + 1 - 2 * core
    owned, width = lat_ref.shape

    loads = [
        pltpu.make_async_copy(lat_hbm, lat_ref, load_sems.at[0]),
        pltpu.make_async_copy(gain_hbm, gain_ref, load_sems.at[1]),
        pltpu.make_async_copy(cot_hbm, cot_ref, load_sems.at[2]),
        pltpu.make_async_copy(w_hbm, w_buf.at[s], load_sems.at[3]),
    ]
    for load in loads:
        load.start()

    barrier = pltpu.get_barrier_semaphore()
    cell = 8 * (s // 8) + 2 * (lax.rem(s, 4) // 2)
    far_desk, near_desk = cell + 1, cell + 5
    cell_members = (cell, cell + 1, cell + 4, cell + 5)

    def loop(lo, hi, act):
        def body(i, carry):
            act(i)
            return carry

        lax.fori_loop(lo, hi, body, 0)

    def greet(q, t):
        pl.semaphore_signal(
            barrier, 1, device_id={"head": q, "ctx": t}, device_id_type=MESH
        )

    def greet_ctx(i):
        @pl.when(2 * i != s)
        def _():
            greet(h, 2 * i)

    loop(0, shards // 2, greet_ctx)
    loop(REACH + 1, heads - REACH, lambda i: greet(lax.rem(h + i, heads), far_desk))
    loop(1, REACH + 1, lambda i: greet(lax.rem(h + i, heads), near_desk))
    loop(1, REACH + 1, lambda i: greet(lax.rem(h + heads - i, heads), near_desk))

    loads[0].wait()
    loads[1].wait()
    raw = lat_ref[...].astype(F32)
    rms = lax.rsqrt(jnp.mean(raw * raw, axis=1, keepdims=True) + 1e-06)
    hat = raw * rms
    gain = gain_ref[...]
    own_n[...] = (hat * gain).astype(BF16)
    n_buf[lax.rem(h, GROUP) * (heads // GROUP) + h // GROUP] = own_n[...]

    def tell(t, go):
        pl.semaphore_signal(
            go, 1, device_id={"head": h, "ctx": t}, device_id_type=MESH
        )

    def gate(desk, expected, listeners, go):
        @pl.when(s == desk)
        def _():
            pl.semaphore_wait(barrier, expected)
            for t in listeners:
                if t is partner:
                    tell(t, go)
                else:
                    pl.when(t != desk)(functools.partial(tell, t, go))

        @pl.when(s != desk)
        def _():
            pl.semaphore_wait(go, 1)

    def send(axis, q, src, dst, lane):
        pltpu.make_async_remote_copy(
            src_ref=src,
            dst_ref=dst,
            send_sem=send_sems.at[lane],
            recv_sem=recv_sems.at[lane],
            device_id={axis: q},
            device_id_type=MESH,
        ).start()

    with jax.named_scope("gate_ctx"):
        gate(s - core, shards - 1, (partner,), ctx_go)
    loads[3].wait()

    def send_w(i):
        send("ctx", lax.rem(s + i, shards), w_buf.at[s], w_buf.at[s], 0)

    loop(1, shards, send_w)

    group, kind = h // GROUP, lax.rem(h, GROUP)
    groups = heads // GROUP
    own_slot = kind * groups + group

    def send_n(j):
        send("head", lax.rem(h + GROUP * j, heads), own_n, n_buf.at[own_slot], 1)

    def far_rows():
        with jax.named_scope("gate_far"):
            gate(far_desk, 4 * (heads - 1 - 2 * REACH), cell_members, far_go)
        loop(REACH // GROUP + 1, groups - REACH // GROUP, send_n)

    late = jnp.logical_and(h >= LATE[0], h < LATE[1])
    pl.when(late)(far_rows)
    loads[2].wait()

    with jax.named_scope("wait_w"):
        drain(w_buf.at[pl.ds(0, shards - 1)], recv_sems.at[0])
    whole = w_buf[...].reshape(width, -1)
    g = lax.dot_general(
        cot_ref[...], whole, (((1,), (1,)), ((), ())), preferred_element_type=F32
    ).astype(BF16)
    for q in range(heads):
        g_send[q] = g[owned * q : owned * (q + 1), :]
    g_recv[h] = g_send[h]

    pl.when(jnp.logical_not(late))(far_rows)
    with jax.named_scope("gate_near"):
        gate(near_desk, 8 * REACH, cell_members, near_go)
    loop(1, REACH // GROUP + 1, send_n)
    loop(groups - REACH // GROUP, groups, send_n)

    def send_g(i):
        off = heads // 2 - i
        q = lax.rem(h + off, heads)
        send("head", q, g_send.at[q], g_recv.at[h], 2)

        @pl.when(off < heads // 2)
        def _():
            r = lax.rem(h + heads - off, heads)
            send("head", r, g_send.at[r], g_recv.at[h], 2)

    loop(0, heads // 2, send_g)

    with jax.named_scope("wait_n1"):
        drain(n_buf.at[pl.ds(0, groups - 1)], recv_sems.at[1])
    mine = n_buf.at[pl.ds(kind * groups, groups)]
    for k in range(GROUP):

        @pl.when(kind != k)
        def _():
            send("head", h - kind + k, mine, mine, 4)

    with jax.named_scope("wait_n2"):
        drain(n_buf.at[pl.ds(0, heads - groups)], recv_sems.at[4])
    for q in range(heads):
        n_mat[owned * q : owned * (q + 1), :] = n_buf[q % GROUP * groups + q // GROUP]
    wg = lax.dot_general(
        n_mat[...], cot_ref[...], (((0,), (0,)), ((), ())), preferred_element_type=F32
    )
    wg_send[...] = wg.astype(BF16).reshape(wg_send.shape)
    wg_recv[s] = wg_send[s]

    def send_wg(i):
        q = lax.rem(s + i, shards)
        send("ctx", q, wg_send.at[q], wg_recv.at[s], 3)

    loop(1, shards, send_wg)

    with jax.named_scope("wait_g"):
        drain(g_recv.at[pl.ds(0, heads - 1)], recv_sems.at[2])
    rows = jnp.sum(g_recv[...].astype(F32), axis=0)
    scaled = rows * gain
    inner = jnp.mean(scaled * hat, axis=1, keepdims=True)
    lg_ref[...] = rms * (scaled - hat * inner)

    with jax.named_scope("wait_wg"):
        drain(wg_recv.at[pl.ds(0, shards - 1)], recv_sems.at[3])
    wg_ref[...] = jnp.sum(wg_recv[...].astype(F32), axis=0).reshape(wg_ref.shape)

    with jax.named_scope("drain"):
        drain(w_buf.at[pl.ds(0, shards - 1)], send_sems.at[0])
        drain(n_buf.at[pl.ds(0, groups - 1)], send_sems.at[1])
        drain(n_buf.at[pl.ds(0, heads - groups)], send_sems.at[4])
        drain(g_send.at[pl.ds(0, heads - 1)], send_sems.at[2])
        drain(wg_send.at[pl.ds(0, shards - 1)], send_sems.at[3])


def solution(mesh):
    heads, shards = mesh.shape["head"], mesh.shape["ctx"]

    def per_device(latent, gain, cotangent, weight):
        _, owned, width = latent.shape
        tokens, channels = cotangent.shape[1], cotangent.shape[3]
        rows = weight.shape[0]
        vmem = pl.BlockSpec(memory_space=pltpu.VMEM)
        lg, wg = pl.pallas_call(
            functools.partial(kernel, heads, shards),
            out_shape=(
                jax.ShapeDtypeStruct((owned, width), F32),
                jax.ShapeDtypeStruct((rows, 1, channels), F32),
            ),
            in_specs=[pl.BlockSpec(memory_space=pl.ANY)] * 4,
            out_specs=(vmem, vmem),
            scratch_shapes=[
                pltpu.VMEM((owned, width), BF16),
                pltpu.VMEM((1, width), F32),
                pltpu.VMEM((tokens, channels), BF16),
                pltpu.VMEM((owned, width), BF16),
                pltpu.VMEM((heads, owned, width), BF16),
                pltpu.VMEM((tokens, width), BF16),
                pltpu.VMEM((shards, rows, channels), BF16),
                pltpu.VMEM((heads, owned, width), BF16),
                pltpu.VMEM((heads, owned, width), BF16),
                pltpu.VMEM((shards, rows, channels), BF16),
                pltpu.VMEM((shards, rows, channels), BF16),
                pltpu.SemaphoreType.DMA((4,)),
                pltpu.SemaphoreType.DMA((5,)),
                pltpu.SemaphoreType.DMA((5,)),
                pltpu.SemaphoreType.REGULAR,
                pltpu.SemaphoreType.REGULAR,
                pltpu.SemaphoreType.REGULAR,
            ],
            compiler_params=pltpu.CompilerParams(collective_id=0, has_side_effects=True),
            name="fused",
        )(
            latent.reshape(owned, width),
            gain.reshape(1, width),
            cotangent.reshape(tokens, channels),
            weight.reshape(rows, channels),
        )
        return lg.reshape(latent.shape), wg.reshape(weight.shape)

    return jax.shard_map(
        per_device,
        mesh=mesh,
        in_specs=(
            P("ctx", "head", None),
            P(),
            P("ctx", None, "head", None),
            P("ctx", "head", None),
        ),
        out_specs=(P("ctx", "head", None), P("ctx", "head", None)),
        check_vma=False,
    )
```

```python
import functools

import jax
import jax.numpy as jnp
from jax import lax
from jax.experimental import pallas as pl
from jax.experimental.pallas import tpu as pltpu
from jax.sharding import PartitionSpec as P

MESH = pl.DeviceIdType.MESH
F32, BF16 = jnp.float32, jnp.bfloat16
GROUP = 4
SPLIT = 28


def drain(ref, sem):
    pltpu.make_async_copy(ref, ref, sem).wait()


def loop(lo, hi, act):
    def body(i, carry):
        act(i)
        return carry

    lax.fori_loop(lo, hi, body, 0)


def kernel(
    heads,
    shards,
    lat_hbm,
    gain_hbm,
    cot_hbm,
    w_hbm,
    lg_ref,
    wg_ref,
    lat_ref,
    gain_ref,
    cot_ref,
    cot_mat,
    own_n,
    n_buf,
    n_mat,
    w_buf,
    g_mat,
    g_send,
    g_near,
    far_send,
    g_far,
    wg_send,
    wg_recv,
    load_sems,
    send_sems,
    recv_sems,
    ctx_go,
    low_go,
    high_go,
):
    h = lax.axis_index("head")
    s = lax.axis_index("ctx")
    core = lax.rem(s, 2)
    partner = s + 1 - 2 * core
    owned, width = lat_ref.shape
    group, kind = h // GROUP, lax.rem(h, GROUP)
    groups = heads // GROUP
    span = groups * owned

    loads = [
        pltpu.make_async_copy(lat_hbm, lat_ref, load_sems.at[0]),
        pltpu.make_async_copy(gain_hbm, gain_ref, load_sems.at[1]),
        pltpu.make_async_copy(cot_hbm, cot_ref, load_sems.at[2]),
        pltpu.make_async_copy(w_hbm, w_buf.at[s], load_sems.at[3]),
    ]
    for load in loads:
        load.start()

    barrier = pltpu.get_barrier_semaphore()
    cell = 8 * (s // 8) + 2 * (lax.rem(s, 4) // 2)
    desks = (cell + 1, cell + 5)
    cell_members = (cell, cell + 1, cell + 4, cell + 5)
    low = h < SPLIT
    my_desk = jnp.where(low, desks[0], desks[1])

    def greet(q, t):
        pl.semaphore_signal(
            barrier, 1, device_id={"head": q, "ctx": t}, device_id_type=MESH
        )

    def greet_ctx(i):
        @pl.when(2 * i != s)
        def _():
            greet(h, 2 * i)

    def alike(j):
        return lax.rem(h + GROUP * j, heads)

    def far_first(act):
        for i in range(groups // 2):
            act(alike(groups // 2 - i))
            if i > 0:
                act(alike(groups // 2 + i))

    def mate(d):
        return h - kind + lax.rem(kind + d, GROUP)

    loop(0, shards // 2, greet_ctx)
    far_first(lambda q: greet(q, my_desk))
    for d in range(1, GROUP):
        greet(mate(d), s - core)

    loads[0].wait()
    loads[1].wait()
    raw = lat_ref[...].astype(F32)
    rms = lax.rsqrt(jnp.mean(raw * raw, axis=1, keepdims=True) + 1e-06)
    hat = raw * rms
    gain = gain_ref[...]
    own_n[...] = (hat * gain).astype(BF16)
    n_buf[group] = own_n[...]

    def tell(t, go):
        pl.semaphore_signal(
            go, 1, device_id={"head": h, "ctx": t}, device_id_type=MESH
        )

    def gate(desk, expected, listeners, go):
        @pl.when(s == desk)
        def _():
            pl.semaphore_wait(barrier, expected)
            for t in listeners:
                if t is partner:
                    tell(t, go)
                else:
                    pl.when(t != desk)(functools.partial(tell, t, go))

        @pl.when(s != desk)
        def _():
            pl.semaphore_wait(go, 1)

    def send(axis, q, src, dst, lane):
        pltpu.make_async_remote_copy(
            src_ref=src,
            dst_ref=dst,
            send_sem=send_sems.at[lane],
            recv_sem=recv_sems.at[lane],
            device_id={axis: q},
            device_id_type=MESH,
        ).start()

    with jax.named_scope("gate_ctx"):
        gate(s - core, shards - 1 + 2 * (GROUP - 1), (partner,), ctx_go)
    loads[3].wait()

    def send_w(i):
        send("ctx", lax.rem(s + i, shards), w_buf.at[s], w_buf.at[s], 0)

    loop(1, shards, send_w)

    def to_low(act):
        far_first(lambda q: pl.when(q < SPLIT)(lambda: act(q)))

    def to_high(act):
        far_first(lambda q: pl.when(q >= SPLIT)(lambda: act(q)))

    def send_n(q):
        send("head", q, own_n, n_buf.at[group], 1)

    def send_far(q):
        send("head", q, far_send.at[q // GROUP], g_far.at[group], 2)

    mine = low.astype(jnp.int32)

    def low_rows():
        with jax.named_scope("gate_low"):
            gate(desks[0], 4 * (SPLIT // GROUP - mine), cell_members, low_go)
        to_low(send_n)

    pl.when(jnp.logical_not(low))(low_rows)

    loads[2].wait()
    for p in range(heads):
        row = (p % GROUP) * span + (p // GROUP) * owned
        cot_mat[row : row + owned, :] = cot_ref[owned * p : owned * (p + 1), :]

    with jax.named_scope("wait_w"):
        drain(w_buf.at[pl.ds(0, shards - 1)], recv_sems.at[0])
    whole = w_buf[...].reshape(width, -1)
    g_mat[...] = lax.dot_general(
        cot_mat[...], whole, (((1,), (1,)), ((), ())), preferred_element_type=F32
    )
    g_send[...] = g_mat[...].astype(BF16).reshape(g_send.shape)
    for d in range(1, GROUP):
        k = lax.rem(kind + d, GROUP)
        send("head", mate(d), g_send.at[k], g_near.at[GROUP - 1 - d], 3)
    with jax.named_scope("wait_near"):
        drain(g_near, recv_sems.at[3])
    part = g_mat[pl.ds(pl.multiple_of(kind * span, span), span), :]
    part = part + jnp.sum(g_near[...].astype(F32), axis=0)
    part = part.astype(BF16)
    for j in range(groups):
        far_send[j] = part[owned * j : owned * (j + 1), :]
    g_far[group] = far_send[group]

    pl.when(low)(low_rows)
    to_low(send_far)
    with jax.named_scope("gate_high"):
        gate(desks[1], 4 * (groups - SPLIT // GROUP - 1 + mine), cell_members, high_go)
    to_high(send_n)
    to_high(send_far)

    with jax.named_scope("wait_n1"):
        drain(n_buf.at[pl.ds(0, groups - 1)], recv_sems.at[1])
    rows = pl.ds(pl.multiple_of(kind * span, span), span)
    mine_n = jnp.concatenate([n_buf[j] for j in range(groups)], axis=0)
    n_mat[rows, :] = mine_n
    for d in range(1, GROUP):
        send("head", mate(d), n_mat.at[rows], n_mat.at[rows], 4)
    with jax.named_scope("wait_n2"):
        drain(n_mat.at[pl.ds(0, (GROUP - 1) * span)], recv_sems.at[4])
    wg = lax.dot_general(
        n_mat[...], cot_mat[...], (((0,), (0,)), ((), ())), preferred_element_type=F32
    )
    wg_send[...] = wg.astype(BF16).reshape(wg_send.shape)
    wg_recv[s] = wg_send[s]

    def send_wg(i):
        q = lax.rem(s + i, shards)
        send("ctx", q, wg_send.at[q], wg_recv.at[s], 5)

    loop(1, shards, send_wg)

    with jax.named_scope("wait_g"):
        drain(g_far.at[pl.ds(0, groups - 1)], recv_sems.at[2])
    scaled = jnp.sum(g_far[...].astype(F32), axis=0) * gain
    inner = jnp.mean(scaled * hat, axis=1, keepdims=True)
    lg_ref[...] = rms * (scaled - hat * inner)

    with jax.named_scope("wait_wg"):
        drain(wg_recv.at[pl.ds(0, shards - 1)], recv_sems.at[5])
    wg_ref[...] = jnp.sum(wg_recv[...].astype(F32), axis=0).reshape(wg_ref.shape)

    with jax.named_scope("drain"):
        drain(w_buf.at[pl.ds(0, shards - 1)], send_sems.at[0])
        drain(n_buf.at[pl.ds(0, groups - 1)], send_sems.at[1])
        drain(g_far.at[pl.ds(0, groups - 1)], send_sems.at[2])
        drain(g_near, send_sems.at[3])
        drain(n_mat.at[pl.ds(0, (GROUP - 1) * span)], send_sems.at[4])
        drain(wg_send.at[pl.ds(0, shards - 1)], send_sems.at[5])


def solution(mesh):
    heads, shards = mesh.shape["head"], mesh.shape["ctx"]

    def per_device(latent, gain, cotangent, weight):
        _, owned, width = latent.shape
        tokens, channels = cotangent.shape[1], cotangent.shape[3]
        rows = weight.shape[0]
        groups = heads // GROUP
        span = groups * owned
        vmem = pl.BlockSpec(memory_space=pltpu.VMEM)
        lg, wg = pl.pallas_call(
            functools.partial(kernel, heads, shards),
            out_shape=(
                jax.ShapeDtypeStruct((owned, width), F32),
                jax.ShapeDtypeStruct((rows, 1, channels), F32),
            ),
            in_specs=[pl.BlockSpec(memory_space=pl.ANY)] * 4,
            out_specs=(vmem, vmem),
            scratch_shapes=[
                pltpu.VMEM((owned, width), BF16),
                pltpu.VMEM((1, width), F32),
                pltpu.VMEM((tokens, channels), BF16),
                pltpu.VMEM((tokens, channels), BF16),
                pltpu.VMEM((owned, width), BF16),
                pltpu.VMEM((groups, owned, width), BF16),
                pltpu.VMEM((tokens, width), BF16),
                pltpu.VMEM((shards, rows, channels), BF16),
                pltpu.VMEM((tokens, width), F32),
                pltpu.VMEM((GROUP, span, width), BF16),
                pltpu.VMEM((GROUP - 1, span, width), BF16),
                pltpu.VMEM((groups, owned, width), BF16),
                pltpu.VMEM((groups, owned, width), BF16),
                pltpu.VMEM((shards, rows, channels), BF16),
                pltpu.VMEM((shards, rows, channels), BF16),
                pltpu.SemaphoreType.DMA((4,)),
                pltpu.SemaphoreType.DMA((6,)),
                pltpu.SemaphoreType.DMA((6,)),
                pltpu.SemaphoreType.REGULAR,
                pltpu.SemaphoreType.REGULAR,
                pltpu.SemaphoreType.REGULAR,
            ],
            compiler_params=pltpu.CompilerParams(collective_id=0, has_side_effects=True),
            name="fused",
        )(
            latent.reshape(owned, width),
            gain.reshape(1, width),
            cotangent.reshape(tokens, channels),
            weight.reshape(rows, channels),
        )
        return lg.reshape(latent.shape), wg.reshape(weight.shape)

    return jax.shard_map(
        per_device,
        mesh=mesh,
        in_specs=(
            P("ctx", "head", None),
            P(),
            P("ctx", None, "head", None),
            P("ctx", "head", None),
        ),
        out_specs=(P("ctx", "head", None), P("ctx", "head", None)),
        check_vma=False,
    )
```

```python
import functools

import jax
import jax.numpy as jnp
from jax import lax
from jax.experimental import pallas as pl
from jax.experimental.pallas import tpu as pltpu
from jax.sharding import PartitionSpec as P

MESH = pl.DeviceIdType.MESH
F32, BF16 = jnp.float32, jnp.bfloat16
GROUP = 4
SPLIT = 16


def drain(ref, sem):
    pltpu.make_async_copy(ref, ref, sem).wait()


def loop(lo, hi, act):
    def body(i, carry):
        act(i)
        return carry

    lax.fori_loop(lo, hi, body, 0)


def kernel(
    heads,
    shards,
    lat_hbm,
    gain_hbm,
    cot_hbm,
    w_hbm,
    lg_ref,
    wg_ref,
    lat_ref,
    gain_ref,
    cot_ref,
    cot_mat,
    own_n,
    n_buf,
    n_mat,
    w_buf,
    g_mat,
    g_send,
    g_near,
    far_send,
    g_far,
    wg_send,
    wg_recv,
    load_sems,
    send_sems,
    recv_sems,
    ctx_go,
    low_go,
    high_go,
):
    h = lax.axis_index("head")
    s = lax.axis_index("ctx")
    core = lax.rem(s, 2)
    partner = s + 1 - 2 * core
    owned, width = lat_ref.shape
    group, kind = h // GROUP, lax.rem(h, GROUP)
    groups = heads // GROUP
    span = groups * owned

    loads = [
        pltpu.make_async_copy(lat_hbm, lat_ref, load_sems.at[0]),
        pltpu.make_async_copy(gain_hbm, gain_ref, load_sems.at[1]),
        pltpu.make_async_copy(cot_hbm, cot_ref, load_sems.at[2]),
        pltpu.make_async_copy(w_hbm, w_buf.at[s], load_sems.at[3]),
    ]
    for load in loads:
        load.start()

    barrier = pltpu.get_barrier_semaphore()
    cell = 8 * (s // 8) + 2 * (lax.rem(s, 4) // 2)
    desks = (cell + 1, cell + 5)
    cell_members = (cell, cell + 1, cell + 4, cell + 5)
    low = h < SPLIT
    my_desk = jnp.where(low, desks[0], desks[1])

    def greet(q, t):
        pl.semaphore_signal(
            barrier, 1, device_id={"head": q, "ctx": t}, device_id_type=MESH
        )

    def greet_ctx(i):
        @pl.when(2 * i != s)
        def _():
            greet(h, 2 * i)

    def alike(j):
        return lax.rem(h + GROUP * j, heads)

    def far_first(act):
        for i in range(groups // 2):
            act(alike(groups // 2 - i))
            if i > 0:
                act(alike(groups // 2 + i))

    def mate(d):
        return h - kind + lax.rem(kind + d, GROUP)

    loop(0, shards // 2, greet_ctx)
    far_first(lambda q: greet(q, my_desk))
    for d in range(1, GROUP):
        greet(mate(d), s - core)

    loads[0].wait()
    loads[1].wait()
    raw = lat_ref[...].astype(F32)
    rms = lax.rsqrt(jnp.mean(raw * raw, axis=1, keepdims=True) + 1e-06)
    hat = raw * rms
    gain = gain_ref[...]
    own_n[...] = (hat * gain).astype(BF16)
    n_buf[group] = own_n[...]

    def tell(t, go):
        pl.semaphore_signal(
            go, 1, device_id={"head": h, "ctx": t}, device_id_type=MESH
        )

    def gate(desk, expected, listeners, go):
        @pl.when(s == desk)
        def _():
            pl.semaphore_wait(barrier, expected)
            for t in listeners:
                if t is partner:
                    tell(t, go)
                else:
                    pl.when(t != desk)(functools.partial(tell, t, go))

        @pl.when(s != desk)
        def _():
            pl.semaphore_wait(go, 1)

    def send(axis, q, src, dst, lane):
        pltpu.make_async_remote_copy(
            src_ref=src,
            dst_ref=dst,
            send_sem=send_sems.at[lane],
            recv_sem=recv_sems.at[lane],
            device_id={axis: q},
            device_id_type=MESH,
        ).start()

    with jax.named_scope("gate_ctx"):
        gate(s - core, shards - 1 + 2 * (GROUP - 1), (partner,), ctx_go)
    loads[3].wait()

    def send_w(i):
        send("ctx", lax.rem(s + i, shards), w_buf.at[s], w_buf.at[s], 0)

    loop(1, shards, send_w)

    def to_low(act):
        far_first(lambda q: pl.when(q < SPLIT)(lambda: act(q)))

    def to_high(act):
        far_first(lambda q: pl.when(q >= SPLIT)(lambda: act(q)))

    def send_n(q):
        send("head", q, own_n, n_buf.at[group], 1)

    def send_far(q):
        send("head", q, far_send.at[q // GROUP], g_far.at[group], 2)

    mine = low.astype(jnp.int32)

    def low_rows():
        with jax.named_scope("gate_low"):
            gate(desks[0], 4 * (SPLIT // GROUP - mine), cell_members, low_go)
        to_low(send_n)

    pl.when(jnp.logical_not(low))(low_rows)

    loads[2].wait()
    for p in range(heads):
        row = (p % GROUP) * span + (p // GROUP) * owned
        cot_mat[row : row + owned, :] = cot_ref[owned * p : owned * (p + 1), :]

    with jax.named_scope("wait_w"):
        drain(w_buf.at[pl.ds(0, shards - 1)], recv_sems.at[0])
    whole = w_buf[...].reshape(width, -1)
    g_mat[...] = lax.dot_general(
        cot_mat[...], whole, (((1,), (1,)), ((), ())), preferred_element_type=F32
    )
    g_send[...] = g_mat[...].astype(BF16).reshape(g_send.shape)
    for d in range(1, GROUP):
        k = lax.rem(kind + d, GROUP)
        send("head", mate(d), g_send.at[k], g_near.at[GROUP - 1 - d], 3)
    with jax.named_scope("wait_near"):
        drain(g_near, recv_sems.at[3])
    part = g_mat[pl.ds(pl.multiple_of(kind * span, span), span), :]
    part = part + jnp.sum(g_near[...].astype(F32), axis=0)
    part = part.astype(BF16)
    for j in range(groups):
        far_send[j] = part[owned * j : owned * (j + 1), :]
    g_far[group] = far_send[group]

    pl.when(low)(low_rows)
    to_low(send_far)
    with jax.named_scope("gate_high"):
        gate(desks[1], 4 * (groups - SPLIT // GROUP - 1 + mine), cell_members, high_go)
    to_high(send_n)
    to_high(send_far)

    with jax.named_scope("wait_n1"):
        drain(n_buf.at[pl.ds(0, groups - 1)], recv_sems.at[1])
    rows = pl.ds(pl.multiple_of(kind * span, span), span)
    mine_n = jnp.concatenate([n_buf[j] for j in range(groups)], axis=0)
    n_mat[rows, :] = mine_n
    for d in range(1, GROUP):
        send("head", mate(d), n_mat.at[rows], n_mat.at[rows], 4)
    with jax.named_scope("wait_n2"):
        drain(n_mat.at[pl.ds(0, (GROUP - 1) * span)], recv_sems.at[4])
    wg = lax.dot_general(
        n_mat[...], cot_mat[...], (((0,), (0,)), ((), ())), preferred_element_type=F32
    )
    wg_send[...] = wg.astype(BF16).reshape(wg_send.shape)
    wg_recv[s] = wg_send[s]

    def send_wg(i):
        q = lax.rem(s + i, shards)
        send("ctx", q, wg_send.at[q], wg_recv.at[s], 5)

    loop(1, shards, send_wg)

    with jax.named_scope("wait_g"):
        drain(g_far.at[pl.ds(0, groups - 1)], recv_sems.at[2])
    scaled = jnp.sum(g_far[...].astype(F32), axis=0) * gain
    inner = jnp.mean(scaled * hat, axis=1, keepdims=True)
    lg_ref[...] = rms * (scaled - hat * inner)

    with jax.named_scope("wait_wg"):
        drain(wg_recv.at[pl.ds(0, shards - 1)], recv_sems.at[5])
    wg_ref[...] = jnp.sum(wg_recv[...].astype(F32), axis=0).reshape(wg_ref.shape)

    with jax.named_scope("drain"):
        drain(w_buf.at[pl.ds(0, shards - 1)], send_sems.at[0])
        drain(n_buf.at[pl.ds(0, groups - 1)], send_sems.at[1])
        drain(g_far.at[pl.ds(0, groups - 1)], send_sems.at[2])
        drain(g_near, send_sems.at[3])
        drain(n_mat.at[pl.ds(0, (GROUP - 1) * span)], send_sems.at[4])
        drain(wg_send.at[pl.ds(0, shards - 1)], send_sems.at[5])


def put(lg_ref, wg_ref, lg_out, wg_out, sems):
    lg = pltpu.make_async_copy(lg_ref, lg_out, sems.at[0])
    wg = pltpu.make_async_copy(wg_ref, wg_out, sems.at[1])
    wg.start()
    lg.start()
    lg.wait()
    wg.wait()


def solution(mesh):
    heads, shards = mesh.shape["head"], mesh.shape["ctx"]

    def per_device(latent, gain, cotangent, weight):
        _, owned, width = latent.shape
        tokens, channels = cotangent.shape[1], cotangent.shape[3]
        rows = weight.shape[0]
        groups = heads // GROUP
        span = groups * owned
        vmem = pl.BlockSpec(memory_space=pltpu.VMEM)
        lg, wg = pl.pallas_call(
            functools.partial(kernel, heads, shards),
            out_shape=(
                pltpu.VMEM((owned, width), F32),
                pltpu.VMEM((rows, 1, channels), F32),
            ),
            in_specs=[pl.BlockSpec(memory_space=pl.ANY)] * 4,
            out_specs=(vmem, vmem),
            scratch_shapes=[
                pltpu.VMEM((owned, width), BF16),
                pltpu.VMEM((1, width), F32),
                pltpu.VMEM((tokens, channels), BF16),
                pltpu.VMEM((tokens, channels), BF16),
                pltpu.VMEM((owned, width), BF16),
                pltpu.VMEM((groups, owned, width), BF16),
                pltpu.VMEM((tokens, width), BF16),
                pltpu.VMEM((shards, rows, channels), BF16),
                pltpu.VMEM((tokens, width), F32),
                pltpu.VMEM((GROUP, span, width), BF16),
                pltpu.VMEM((GROUP - 1, span, width), BF16),
                pltpu.VMEM((groups, owned, width), BF16),
                pltpu.VMEM((groups, owned, width), BF16),
                pltpu.VMEM((shards, rows, channels), BF16),
                pltpu.VMEM((shards, rows, channels), BF16),
                pltpu.SemaphoreType.DMA((4,)),
                pltpu.SemaphoreType.DMA((6,)),
                pltpu.SemaphoreType.DMA((6,)),
                pltpu.SemaphoreType.REGULAR,
                pltpu.SemaphoreType.REGULAR,
                pltpu.SemaphoreType.REGULAR,
            ],
            compiler_params=pltpu.CompilerParams(collective_id=0, has_side_effects=True),
            name="fused",
        )(
            latent.reshape(owned, width),
            gain.reshape(1, width),
            cotangent.reshape(tokens, channels),
            weight.reshape(rows, channels),
        )
        lg, wg = pl.pallas_call(
            put,
            out_shape=(
                jax.ShapeDtypeStruct((owned, width), F32),
                jax.ShapeDtypeStruct((rows, 1, channels), F32),
            ),
            in_specs=[vmem, vmem],
            out_specs=(pl.BlockSpec(memory_space=pl.ANY), pl.BlockSpec(memory_space=pl.ANY)),
            scratch_shapes=[pltpu.SemaphoreType.DMA((2,))],
            name="put",
        )(
            pltpu.with_memory_space_constraint(lg, pltpu.VMEM),
            pltpu.with_memory_space_constraint(wg, pltpu.VMEM),
        )
        return lg.reshape(latent.shape), wg.reshape(weight.shape)

    return jax.shard_map(
        per_device,
        mesh=mesh,
        in_specs=(
            P("ctx", "head", None),
            P(),
            P("ctx", None, "head", None),
            P("ctx", "head", None),
        ),
        out_specs=(P("ctx", "head", None), P("ctx", "head", None)),
        check_vma=False,
    )
```

```python
import functools

import jax
import jax.numpy as jnp
from jax import lax
from jax.experimental import pallas as pl
from jax.experimental.pallas import tpu as pltpu
from jax.sharding import PartitionSpec as P

MESH = pl.DeviceIdType.MESH
F32, BF16 = jnp.float32, jnp.bfloat16
GROUP = 4
SUB = 8
SPLIT = 16


def drain(ref, sem):
    pltpu.make_async_copy(ref, ref, sem).wait()


def loop(lo, hi, act):
    def body(i, carry):
        act(i)
        return carry

    lax.fori_loop(lo, hi, body, 0)


def kernel(
    heads,
    shards,
    lat_hbm,
    gain_hbm,
    cot_hbm,
    w_hbm,
    lg_ref,
    wg_ref,
    lat_ref,
    gain_ref,
    cot_ref,
    cot_all,
    own_n,
    n_buf,
    w_buf,
    g_mat,
    g_send,
    g_near,
    far_send,
    g_far,
    pk_send,
    pk_recv,
    load_sems,
    send_sems,
    recv_sems,
    ctx_go,
    low_go,
    high_go,
):
    h = lax.axis_index("head")
    s = lax.axis_index("ctx")
    core = lax.rem(s, 2)
    partner = s + 1 - 2 * core
    owned, width = lat_ref.shape
    group, kind = h // GROUP, lax.rem(h, GROUP)
    groups = heads // GROUP
    span = groups * owned
    blocks = span // SUB

    loads = [
        pltpu.make_async_copy(lat_hbm, lat_ref, load_sems.at[0]),
        pltpu.make_async_copy(gain_hbm, gain_ref, load_sems.at[1]),
        pltpu.make_async_copy(cot_hbm, cot_ref, load_sems.at[2]),
        pltpu.make_async_copy(w_hbm, w_buf.at[s], load_sems.at[3]),
    ]
    for load in loads:
        load.start()

    barrier = pltpu.get_barrier_semaphore()
    cell = 8 * (s // 8) + 2 * (lax.rem(s, 4) // 2)
    desks = (cell + 1, cell + 5)
    cell_members = (cell, cell + 1, cell + 4, cell + 5)
    low = h < SPLIT
    my_desk = jnp.where(low, desks[0], desks[1])

    def greet(q, t):
        pl.semaphore_signal(
            barrier, 1, device_id={"head": q, "ctx": t}, device_id_type=MESH
        )

    def greet_ctx(i):
        @pl.when(2 * i != s)
        def _():
            greet(h, 2 * i)

    def alike(j):
        return lax.rem(h + GROUP * j, heads)

    def far_first(act):
        for i in range(groups // 2):
            act(alike(groups // 2 - i))
            if i > 0:
                act(alike(groups // 2 + i))

    def mate(d):
        return h - kind + lax.rem(kind + d, GROUP)

    loop(0, shards // 2, greet_ctx)
    far_first(lambda q: greet(q, my_desk))
    for d in range(1, GROUP):
        greet(mate(d), s - core)

    loads[0].wait()
    loads[1].wait()
    raw = lat_ref[...].astype(F32)
    rms = lax.rsqrt(jnp.mean(raw * raw, axis=1, keepdims=True) + 1e-06)
    hat = raw * rms
    gain = gain_ref[...]
    own_n[...] = (hat * gain).astype(BF16)
    n_buf[group] = own_n[...]

    def tell(t, go):
        pl.semaphore_signal(
            go, 1, device_id={"head": h, "ctx": t}, device_id_type=MESH
        )

    def gate(desk, expected, listeners, go):
        @pl.when(s == desk)
        def _():
            pl.semaphore_wait(barrier, expected)
            for t in listeners:
                if t is partner:
                    tell(t, go)
                else:
                    pl.when(t != desk)(functools.partial(tell, t, go))

        @pl.when(s != desk)
        def _():
            pl.semaphore_wait(go, 1)

    def send(axis, q, src, dst, lane):
        pltpu.make_async_remote_copy(
            src_ref=src,
            dst_ref=dst,
            send_sem=send_sems.at[lane],
            recv_sem=recv_sems.at[lane],
            device_id={axis: q},
            device_id_type=MESH,
        ).start()

    with jax.named_scope("gate_ctx"):
        gate(s - core, shards - 1 + 2 * (GROUP - 1), (partner,), ctx_go)
    loads[3].wait()

    def send_ctx(i, src, dst, lane):
        q = lax.rem(s + i, shards)
        send("ctx", q, src(q), dst, lane)

    loop(1, shards, lambda i: send_ctx(i, lambda q: w_buf.at[s], w_buf.at[s], 0))

    def to_low(act):
        far_first(lambda q: pl.when(q < SPLIT)(lambda: act(q)))

    def to_high(act):
        far_first(lambda q: pl.when(q >= SPLIT)(lambda: act(q)))

    def send_n(q):
        send("head", q, own_n, n_buf.at[group], 1)

    def send_far(q):
        send("head", q, far_send.at[q // GROUP], g_far.at[group], 2)

    mine = low.astype(jnp.int32)

    def low_rows():
        with jax.named_scope("gate_low"):
            gate(desks[0], 4 * (SPLIT // GROUP - mine), cell_members, low_go)
        to_low(send_n)

    pl.when(jnp.logical_not(low))(low_rows)

    loads[2].wait()
    cot_mat = cot_all.at[s]
    for p in range(heads):
        at = p // GROUP * owned
        row = (at // SUB * GROUP + p % GROUP) * SUB + at % SUB
        cot_mat[row : row + owned, :] = cot_ref[owned * p : owned * (p + 1), :]

    with jax.named_scope("wait_w"):
        drain(w_buf.at[pl.ds(0, shards - 1)], recv_sems.at[0])
    whole = w_buf[...].reshape(width, -1)
    g = lax.dot_general(
        cot_mat[...], whole, (((1,), (1,)), ((), ())), preferred_element_type=F32
    )
    for k in range(GROUP):
        starts = [(b * GROUP + k) * SUB for b in range(blocks)]
        g_k = jnp.concatenate([g[r : r + SUB, :] for r in starts], axis=0)
        g_mat[k] = g_k
        g_send[k] = g_k.astype(BF16)
    for d in range(1, GROUP):
        k = lax.rem(kind + d, GROUP)
        send("head", mate(d), g_send.at[k], g_near.at[GROUP - 1 - d], 3)
    with jax.named_scope("wait_near"):
        drain(g_near, recv_sems.at[3])
    part = g_mat[kind] + jnp.sum(g_near[...].astype(F32), axis=0)
    part = part.astype(BF16)
    for j in range(groups):
        far_send[j] = part[owned * j : owned * (j + 1), :]
    g_far[group] = far_send[group]

    def send_cot():
        loop(1, shards, lambda i: send_ctx(i, lambda q: cot_all.at[s], cot_all.at[s], 5))

    @pl.when(low)
    def _():
        send_cot()
        low_rows()

    to_low(send_far)
    with jax.named_scope("gate_high"):
        gate(desks[1], 4 * (groups - SPLIT // GROUP - 1 + mine), cell_members, high_go)
    to_high(send_n)
    to_high(send_far)
    pl.when(jnp.logical_not(low))(send_cot)

    with jax.named_scope("wait_n1"):
        drain(n_buf.at[pl.ds(0, groups - 1)], recv_sems.at[1])
    rows = jnp.concatenate([n_buf[j].astype(F32) for j in range(groups)], axis=0)
    strip = width // shards
    lanes = strip * blocks
    lane_block = lax.broadcasted_iota(jnp.int32, (SUB, lanes), 1) // strip
    for q in range(shards):
        base, turn = q * strip // lanes * lanes, q * strip % lanes
        packed = None
        for b in range(blocks):
            tile = rows[b * SUB : (b + 1) * SUB, base : base + lanes]
            shift = (b * strip - turn) % lanes
            tile = pltpu.roll(tile, shift, 1) if shift else tile
            packed = tile if b == 0 else jnp.where(lane_block == b, tile, packed)
        pk_send[q] = packed.astype(BF16)
    slot = s * GROUP + kind
    pk_recv[slot] = pk_send[s]

    def send_pk(i):
        q = lax.rem(s + shards - i, shards)
        for d in (3, 1, 2, 0):

            @pl.when(jnp.logical_or(i > 0, d > 0))
            def _():
                pltpu.make_async_remote_copy(
                    src_ref=pk_send.at[q],
                    dst_ref=pk_recv.at[slot],
                    send_sem=send_sems.at[4],
                    recv_sem=recv_sems.at[4],
                    device_id={"head": mate(d), "ctx": q},
                    device_id_type=MESH,
                ).start()

    loop(0, shards, send_pk)
    with jax.named_scope("wait_cot"):
        drain(cot_all.at[pl.ds(0, shards - 1)], recv_sems.at[5])
    with jax.named_scope("wait_pk"):
        drain(pk_recv.at[pl.ds(0, GROUP * shards - 1)], recv_sems.at[4])
    strips = pk_recv[...].astype(F32).reshape(-1, lanes).T.astype(BF16)
    wg = jnp.zeros((strip, w_buf.shape[2]), F32)
    for b in range(blocks):
        cot_b = cot_all[:, b * GROUP * SUB : (b + 1) * GROUP * SUB, :]
        wg = wg + lax.dot_general(
            strips[b * strip : (b + 1) * strip, :],
            cot_b.reshape(-1, cot_b.shape[2]),
            (((1,), (0,)), ((), ())),
            preferred_element_type=F32,
        )
    wg_ref[...] = wg.reshape(wg_ref.shape)

    with jax.named_scope("wait_g"):
        drain(g_far.at[pl.ds(0, groups - 1)], recv_sems.at[2])
    scaled = jnp.sum(g_far[...].astype(F32), axis=0) * gain
    inner = jnp.mean(scaled * hat, axis=1, keepdims=True)
    lg_ref[...] = rms * (scaled - hat * inner)

    with jax.named_scope("drain"):
        drain(w_buf.at[pl.ds(0, shards - 1)], send_sems.at[0])
        drain(n_buf.at[pl.ds(0, groups - 1)], send_sems.at[1])
        drain(g_far.at[pl.ds(0, groups - 1)], send_sems.at[2])
        drain(g_near, send_sems.at[3])
        drain(pk_recv.at[pl.ds(0, GROUP * shards - 1)], send_sems.at[4])
        drain(cot_all.at[pl.ds(0, shards - 1)], send_sems.at[5])


def put(lg_ref, wg_ref, lg_out, wg_out, sems):
    lg = pltpu.make_async_copy(lg_ref, lg_out, sems.at[0])
    wg = pltpu.make_async_copy(wg_ref, wg_out, sems.at[1])
    wg.start()
    lg.start()
    lg.wait()
    wg.wait()


def solution(mesh):
    heads, shards = mesh.shape["head"], mesh.shape["ctx"]

    def per_device(latent, gain, cotangent, weight):
        _, owned, width = latent.shape
        tokens, channels = cotangent.shape[1], cotangent.shape[3]
        rows = weight.shape[0]
        groups = heads // GROUP
        span = groups * owned
        vmem = pl.BlockSpec(memory_space=pltpu.VMEM)
        lg, wg = pl.pallas_call(
            functools.partial(kernel, heads, shards),
            out_shape=(
                pltpu.VMEM((owned, width), F32),
                pltpu.VMEM((rows, 1, channels), F32),
            ),
            in_specs=[pl.BlockSpec(memory_space=pl.ANY)] * 4,
            out_specs=(vmem, vmem),
            scratch_shapes=[
                pltpu.VMEM((owned, width), BF16),
                pltpu.VMEM((1, width), F32),
                pltpu.VMEM((tokens, channels), BF16),
                pltpu.VMEM((shards, tokens, channels), BF16),
                pltpu.VMEM((owned, width), BF16),
                pltpu.VMEM((groups, owned, width), BF16),
                pltpu.VMEM((shards, rows, channels), BF16),
                pltpu.VMEM((GROUP, span, width), F32),
                pltpu.VMEM((GROUP, span, width), BF16),
                pltpu.VMEM((GROUP - 1, span, width), BF16),
                pltpu.VMEM((groups, owned, width), BF16),
                pltpu.VMEM((groups, owned, width), BF16),
                pltpu.VMEM((shards, SUB, width // shards * span // SUB), BF16),
                pltpu.VMEM((GROUP * shards, SUB, width // shards * span // SUB), BF16),
                pltpu.SemaphoreType.DMA((4,)),
                pltpu.SemaphoreType.DMA((6,)),
                pltpu.SemaphoreType.DMA((6,)),
                pltpu.SemaphoreType.REGULAR,
                pltpu.SemaphoreType.REGULAR,
                pltpu.SemaphoreType.REGULAR,
            ],
            compiler_params=pltpu.CompilerParams(collective_id=0, has_side_effects=True),
            name="fused",
        )(
            latent.reshape(owned, width),
            gain.reshape(1, width),
            cotangent.reshape(tokens, channels),
            weight.reshape(rows, channels),
        )
        lg, wg = pl.pallas_call(
            put,
            out_shape=(
                jax.ShapeDtypeStruct((owned, width), F32),
                jax.ShapeDtypeStruct((rows, 1, channels), F32),
            ),
            in_specs=[vmem, vmem],
            out_specs=(pl.BlockSpec(memory_space=pl.ANY), pl.BlockSpec(memory_space=pl.ANY)),
            scratch_shapes=[pltpu.SemaphoreType.DMA((2,))],
            name="put",
        )(
            pltpu.with_memory_space_constraint(lg, pltpu.VMEM),
            pltpu.with_memory_space_constraint(wg, pltpu.VMEM),
        )
        return lg.reshape(latent.shape), wg.reshape(weight.shape)

    return jax.shard_map(
        per_device,
        mesh=mesh,
        in_specs=(
            P("ctx", "head", None),
            P(),
            P("ctx", None, "head", None),
            P("ctx", "head", None),
        ),
        out_specs=(P("ctx", "head", None), P("ctx", "head", None)),
        check_vma=False,
    )
```

```python
import functools

import jax
import jax.numpy as jnp
from jax import lax
from jax.experimental import pallas as pl
from jax.experimental.pallas import tpu as pltpu
from jax.sharding import PartitionSpec as P

MESH = pl.DeviceIdType.MESH
F32, BF16 = jnp.float32, jnp.bfloat16
GROUP = 4
SUB = 8
SPLIT = 16
TURNS = tuple((dx, dy, dc) for dx in (2, 1, 3, 0) for dy in (1, 0) for dc in (0, 1) if dx or dy or dc)


def drain(ref, sem):
    pltpu.make_async_copy(ref, ref, sem).wait()


def loop(lo, hi, act):
    def body(i, carry):
        act(i)
        return carry

    lax.fori_loop(lo, hi, body, 0)


def kernel(
    heads,
    shards,
    lat_hbm,
    gain_hbm,
    cot_hbm,
    w_hbm,
    lg_ref,
    wg_ref,
    lat_ref,
    gain_ref,
    cot_ref,
    cot_all,
    own_n,
    n_buf,
    w_buf,
    g_mat,
    g_send,
    g_near,
    far_send,
    g_far,
    dir_send,
    g_dir,
    pk_send,
    pk_recv,
    load_sems,
    send_sems,
    recv_sems,
    ctx_go,
    low_go,
    high_go,
):
    h = lax.axis_index("head")
    s = lax.axis_index("ctx")
    core = lax.rem(s, 2)
    partner = s + 1 - 2 * core
    owned, width = lat_ref.shape
    group, kind = h // GROUP, lax.rem(h, GROUP)
    groups = heads // GROUP
    span = groups * owned
    blocks = span // SUB

    loads = [
        pltpu.make_async_copy(lat_hbm, lat_ref, load_sems.at[0]),
        pltpu.make_async_copy(gain_hbm, gain_ref, load_sems.at[1]),
        pltpu.make_async_copy(cot_hbm, cot_ref, load_sems.at[2]),
        pltpu.make_async_copy(w_hbm, w_buf.at[s], load_sems.at[3]),
    ]
    for load in loads:
        load.start()

    barrier = pltpu.get_barrier_semaphore()
    cell = 8 * (s // 8) + 2 * (lax.rem(s, 4) // 2)
    desks = (cell + 1, cell + 5)
    cell_members = (cell, cell + 1, cell + 4, cell + 5)
    low = h < SPLIT
    my_desk = jnp.where(low, desks[0], desks[1])

    def greet(q, t):
        pl.semaphore_signal(
            barrier, 1, device_id={"head": q, "ctx": t}, device_id_type=MESH
        )

    low_groups, half = SPLIT // GROUP, groups // 2

    def direct(t):
        gap = lax.rem(group - t + groups, groups)
        return jnp.logical_and(gap >= half - 1, gap <= half + 1)

    n_direct = sum(direct(t).astype(jnp.int32) for t in range(low_groups))

    def greet_ctx(i):
        @pl.when(2 * i != s)
        def _():
            greet(h, 2 * i)

    def alike(j):
        return lax.rem(h + GROUP * j, heads)

    def far_first(act):
        for i in range(groups // 2):
            act(alike(groups // 2 - i))
            if i > 0:
                act(alike(groups // 2 + i))

    mate_kind = {0: kind, 1: kind + 1 - 2 * lax.rem(kind, 2), 2: lax.rem(kind + 2, GROUP), 3: GROUP - 1 - kind}

    def mate(d):
        return h - kind + mate_kind[d]

    loop(0, shards // 2, greet_ctx)
    far_first(lambda q: greet(q, my_desk))
    for d in range(1, GROUP):
        greet(mate(d), s - core)

    @pl.when(low)
    def _():
        for j in (half, half + 1, half - 1):
            for d in range(1, GROUP):
                greet(lax.rem(mate(d) + GROUP * j, heads), my_desk)
            g_far[lax.rem(group + j, groups)] = jnp.zeros((owned, width), BF16)

    @pl.when(jnp.logical_not(low))
    def _():
        g_dir[...] = jnp.zeros_like(g_dir)

    loads[0].wait()
    loads[1].wait()
    raw = lat_ref[...].astype(F32)
    rms = lax.rsqrt(jnp.mean(raw * raw, axis=1, keepdims=True) + 1e-06)
    hat = raw * rms
    gain = gain_ref[...]
    own_n[...] = (hat * gain).astype(BF16)
    n_buf[group] = own_n[...]

    def peer(dx, dy, dc):
        x, y = lax.rem(s // 4 + dx, 4), lax.rem(s // 2 + dy, 2)
        return 4 * x + 2 * y + lax.rem(core + dc, 2)

    def tell(t, go):
        pl.semaphore_signal(
            go, 1, device_id={"head": h, "ctx": t}, device_id_type=MESH
        )

    def gate(desk, expected, listeners, go):
        @pl.when(s == desk)
        def _():
            pl.semaphore_wait(barrier, expected)
            for t in listeners:
                if t is partner:
                    tell(t, go)
                else:
                    pl.when(t != desk)(functools.partial(tell, t, go))

        @pl.when(s != desk)
        def _():
            pl.semaphore_wait(go, 1)

    def send(axis, q, src, dst, lane):
        pltpu.make_async_remote_copy(
            src_ref=src,
            dst_ref=dst,
            send_sem=send_sems.at[lane],
            recv_sem=recv_sems.at[lane],
            device_id={axis: q},
            device_id_type=MESH,
        ).start()

    with jax.named_scope("gate_ctx"):
        gate(s - core, shards - 1 + 2 * (GROUP - 1), (partner,), ctx_go)
    loads[3].wait()

    def send_ctx(i, src, dst, lane):
        q = lax.rem(s + i, shards)
        send("ctx", q, src(q), dst, lane)

    for turn in TURNS:
        send("ctx", peer(*turn), w_buf.at[s], w_buf.at[s], 0)

    def to_low(act):
        far_first(lambda q: pl.when(q < SPLIT)(lambda: act(q)))

    def to_high(act):
        far_first(lambda q: pl.when(q >= SPLIT)(lambda: act(q)))

    def send_n(q):
        send("head", q, own_n, n_buf.at[group], 1)

    def send_far(q):
        send("head", q, far_send.at[q // GROUP], g_far.at[group], 2)

    def send_cot():
        loop(1, shards, lambda i: send_ctx(i, lambda q: cot_all.at[s], cot_all.at[s], 5))

    mine = low.astype(jnp.int32)

    def low_rows():
        with jax.named_scope("gate_low"):
            expected = 4 * (low_groups - mine + (GROUP - 1) * n_direct)
            gate(desks[0], expected, cell_members, low_go)
        to_low(send_n)

    pl.when(jnp.logical_not(low))(low_rows)

    loads[2].wait()
    cot_mat = cot_all.at[s]
    for p in range(heads):
        at = p // GROUP * owned
        row = (at // SUB * GROUP + p % GROUP) * SUB + at % SUB
        cot_mat[row : row + owned, :] = cot_ref[owned * p : owned * (p + 1), :]

    pl.when(low)(send_cot)

    with jax.named_scope("wait_w"):
        drain(w_buf.at[pl.ds(0, shards - 1)], recv_sems.at[0])
    whole = w_buf[...].reshape(width, -1)
    g = lax.dot_general(
        cot_mat[...], whole, (((1,), (1,)), ((), ())), preferred_element_type=F32
    )
    for k in range(GROUP):
        starts = [(b * GROUP + k) * SUB for b in range(blocks)]
        g_k = jnp.concatenate([g[r : r + SUB, :] for r in starts], axis=0)
        g_mat[k] = g_k
        g_send[k] = g_k.astype(BF16)
    for d in (3, 1, 2):
        send("head", mate(d), g_send.at[mate_kind[d]], g_near.at[d - 1], 3)
    for t in range(low_groups):
        for k in range(GROUP):
            r = (owned * t // SUB * GROUP + k) * SUB + owned * t % SUB
            dir_send[GROUP * t + k] = g[r : r + owned, :].astype(BF16)
        slot = (lax.rem(group - t + groups, groups) - half + 1) * GROUP + kind

        @pl.when(direct(t))
        def _():
            for k in range(GROUP):
                q = GROUP * t + k
                send("head", q, dir_send.at[q], g_dir.at[slot], 6)

    pl.when(low)(low_rows)

    with jax.named_scope("wait_near"):
        drain(g_near, recv_sems.at[3])
    part = g_mat[kind] + jnp.sum(g_near[...].astype(F32), axis=0)
    part = part.astype(BF16)
    for j in range(groups):
        far_send[j] = part[owned * j : owned * (j + 1), :]
    g_far[group] = far_send[group]

    to_low(lambda q: pl.when(jnp.logical_not(direct(q // GROUP)))(lambda: send_far(q)))
    with jax.named_scope("gate_high"):
        gate(desks[1], 4 * (groups - low_groups - 1 + mine), cell_members, high_go)
    to_high(send_n)
    to_high(send_far)
    pl.when(jnp.logical_not(low))(send_cot)

    with jax.named_scope("wait_n1"):
        drain(n_buf.at[pl.ds(0, groups - 1)], recv_sems.at[1])
    rows = jnp.concatenate([n_buf[j].astype(F32) for j in range(groups)], axis=0)
    strip = width // shards
    lanes = strip * blocks
    lane_block = lax.broadcasted_iota(jnp.int32, (SUB, lanes), 1) // strip
    for q in range(shards):
        base, turn = q * strip // lanes * lanes, q * strip % lanes
        packed = None
        for b in range(blocks):
            tile = rows[b * SUB : (b + 1) * SUB, base : base + lanes]
            shift = (b * strip - turn) % lanes
            tile = pltpu.roll(tile, shift, 1) if shift else tile
            packed = tile if b == 0 else jnp.where(lane_block == b, tile, packed)
        pk_send[q] = packed.astype(BF16)
    slot = s * GROUP + kind
    pk_recv[slot] = pk_send[s]

    for dx, dy, dc in TURNS + ((0, 0, 0),):
        q = peer(dx, dy, dc)
        for d in (3, 1, 2, 0):
            if dx or dy or dc or d:
                pltpu.make_async_remote_copy(
                    src_ref=pk_send.at[q],
                    dst_ref=pk_recv.at[slot],
                    send_sem=send_sems.at[4],
                    recv_sem=recv_sems.at[4],
                    device_id={"head": mate(d), "ctx": q},
                    device_id_type=MESH,
                ).start()

    with jax.named_scope("wait_g"):

        @pl.when(low)
        def _():
            drain(g_far.at[pl.ds(0, groups - 4)], recv_sems.at[2])
            drain(g_dir, recv_sems.at[6])

        @pl.when(jnp.logical_not(low))
        def _():
            drain(g_far.at[pl.ds(0, groups - 1)], recv_sems.at[2])

    total = jnp.sum(g_far[...].astype(F32), axis=0) + jnp.sum(g_dir[...].astype(F32), axis=0)
    scaled = total * gain
    inner = jnp.mean(scaled * hat, axis=1, keepdims=True)
    lg_ref[...] = rms * (scaled - hat * inner)

    with jax.named_scope("wait_cot"):
        drain(cot_all.at[pl.ds(0, shards - 1)], recv_sems.at[5])
    with jax.named_scope("wait_pk"):
        drain(pk_recv.at[pl.ds(0, GROUP * shards - 1)], recv_sems.at[4])
    strips = pk_recv[...].astype(F32).reshape(-1, lanes).T.astype(BF16)
    wg = jnp.zeros((strip, w_buf.shape[2]), F32)
    for b in range(blocks):
        cot_b = cot_all[:, b * GROUP * SUB : (b + 1) * GROUP * SUB, :]
        wg = wg + lax.dot_general(
            strips[b * strip : (b + 1) * strip, :],
            cot_b.reshape(-1, cot_b.shape[2]),
            (((1,), (0,)), ((), ())),
            preferred_element_type=F32,
        )
    wg_ref[...] = wg.reshape(wg_ref.shape)

    with jax.named_scope("drain"):
        drain(w_buf.at[pl.ds(0, shards - 1)], send_sems.at[0])
        drain(n_buf.at[pl.ds(0, groups - 1)], send_sems.at[1])
        for n in range(4):

            @pl.when(n_direct == n)
            def _():
                drain(g_far.at[pl.ds(0, groups - 1 - n)], send_sems.at[2])
                if n:
                    drain(g_dir.at[pl.ds(0, GROUP * n)], send_sems.at[6])

        drain(g_near, send_sems.at[3])
        drain(pk_recv.at[pl.ds(0, GROUP * shards - 1)], send_sems.at[4])
        drain(cot_all.at[pl.ds(0, shards - 1)], send_sems.at[5])


def put(lg_ref, wg_ref, lg_out, wg_out, sems):
    lg = pltpu.make_async_copy(lg_ref, lg_out, sems.at[0])
    wg = pltpu.make_async_copy(wg_ref, wg_out, sems.at[1])
    wg.start()
    lg.start()
    lg.wait()
    wg.wait()


def solution(mesh):
    heads, shards = mesh.shape["head"], mesh.shape["ctx"]

    def per_device(latent, gain, cotangent, weight):
        _, owned, width = latent.shape
        tokens, channels = cotangent.shape[1], cotangent.shape[3]
        rows = weight.shape[0]
        groups = heads // GROUP
        span = groups * owned
        vmem = pl.BlockSpec(memory_space=pltpu.VMEM)
        lg, wg = pl.pallas_call(
            functools.partial(kernel, heads, shards),
            out_shape=(
                pltpu.VMEM((owned, width), F32),
                pltpu.VMEM((rows, 1, channels), F32),
            ),
            in_specs=[pl.BlockSpec(memory_space=pl.ANY)] * 4,
            out_specs=(vmem, vmem),
            scratch_shapes=[
                pltpu.VMEM((owned, width), BF16),
                pltpu.VMEM((1, width), F32),
                pltpu.VMEM((tokens, channels), BF16),
                pltpu.VMEM((shards, tokens, channels), BF16),
                pltpu.VMEM((owned, width), BF16),
                pltpu.VMEM((groups, owned, width), BF16),
                pltpu.VMEM((shards, rows, channels), BF16),
                pltpu.VMEM((GROUP, span, width), F32),
                pltpu.VMEM((GROUP, span, width), BF16),
                pltpu.VMEM((GROUP - 1, span, width), BF16),
                pltpu.VMEM((groups, owned, width), BF16),
                pltpu.VMEM((groups, owned, width), BF16),
                pltpu.VMEM((SPLIT, owned, width), BF16),
                pltpu.VMEM((3 * GROUP, owned, width), BF16),
                pltpu.VMEM((shards, SUB, width // shards * span // SUB), BF16),
                pltpu.VMEM((GROUP * shards, SUB, width // shards * span // SUB), BF16),
                pltpu.SemaphoreType.DMA((4,)),
                pltpu.SemaphoreType.DMA((7,)),
                pltpu.SemaphoreType.DMA((7,)),
                pltpu.SemaphoreType.REGULAR,
                pltpu.SemaphoreType.REGULAR,
                pltpu.SemaphoreType.REGULAR,
            ],
            compiler_params=pltpu.CompilerParams(collective_id=0, has_side_effects=True),
            name="fused",
        )(
            latent.reshape(owned, width),
            gain.reshape(1, width),
            cotangent.reshape(tokens, channels),
            weight.reshape(rows, channels),
        )
        lg, wg = pl.pallas_call(
            put,
            out_shape=(
                jax.ShapeDtypeStruct((owned, width), F32),
                jax.ShapeDtypeStruct((rows, 1, channels), F32),
            ),
            in_specs=[vmem, vmem],
            out_specs=(pl.BlockSpec(memory_space=pl.ANY), pl.BlockSpec(memory_space=pl.ANY)),
            scratch_shapes=[pltpu.SemaphoreType.DMA((2,))],
            name="put",
        )(
            pltpu.with_memory_space_constraint(lg, pltpu.VMEM),
            pltpu.with_memory_space_constraint(wg, pltpu.VMEM),
        )
        return lg.reshape(latent.shape), wg.reshape(weight.shape)

    return jax.shard_map(
        per_device,
        mesh=mesh,
        in_specs=(
            P("ctx", "head", None),
            P(),
            P("ctx", None, "head", None),
            P("ctx", "head", None),
        ),
        out_specs=(P("ctx", "head", None), P("ctx", "head", None)),
        check_vma=False,
    )
```

```python
import functools

import jax
import jax.numpy as jnp
from jax import lax
from jax.experimental import pallas as pl
from jax.experimental.pallas import tpu as pltpu
from jax.sharding import PartitionSpec as P

MESH = pl.DeviceIdType.MESH
F32, BF16 = jnp.float32, jnp.bfloat16
GROUP = 4
SUB = 8
SPLIT = 16
TURNS = tuple((dx, dy, dc) for dx in (2, 1, 3, 0) for dy in (1, 0) for dc in (0, 1) if dx or dy or dc)


def drain(ref, sem):
    pltpu.make_async_copy(ref, ref, sem).wait()


def loop(lo, hi, act):
    def body(i, carry):
        act(i)
        return carry

    lax.fori_loop(lo, hi, body, 0)


def kernel(
    heads,
    shards,
    lat_hbm,
    gain_hbm,
    cot_hbm,
    w_hbm,
    lg_ref,
    wg_ref,
    lat_ref,
    gain_ref,
    cot_ref,
    cot_all,
    own_n,
    n_buf,
    w_buf,
    g_mat,
    g_send,
    g_near,
    far_send,
    g_far,
    dir_send,
    g_dir,
    pk_send,
    pk_recv,
    load_sems,
    send_sems,
    recv_sems,
    ctx_go,
    low_go,
    high_go,
):
    h = lax.axis_index("head")
    s = lax.axis_index("ctx")
    core = lax.rem(s, 2)
    partner = s + 1 - 2 * core
    owned, width = lat_ref.shape
    group, kind = h // GROUP, lax.rem(h, GROUP)
    groups = heads // GROUP
    span = groups * owned
    blocks = span // SUB

    loads = [
        pltpu.make_async_copy(lat_hbm, lat_ref, load_sems.at[0]),
        pltpu.make_async_copy(gain_hbm, gain_ref, load_sems.at[1]),
        pltpu.make_async_copy(cot_hbm, cot_ref, load_sems.at[2]),
        pltpu.make_async_copy(w_hbm, w_buf.at[s], load_sems.at[3]),
    ]
    barrier = pltpu.get_barrier_semaphore()
    cell = 8 * (s // 8) + 2 * (lax.rem(s, 4) // 2)
    desks = (cell + 1, cell + 5)
    cell_members = (cell, cell + 1, cell + 4, cell + 5)
    low = h < SPLIT
    my_desk = jnp.where(low, desks[0], desks[1])

    def greet(q, t):
        pl.semaphore_signal(
            barrier, 1, device_id={"head": q, "ctx": t}, device_id_type=MESH
        )

    low_groups, half = SPLIT // GROUP, groups // 2

    def direct(t):
        gap = lax.rem(group - t + groups, groups)
        return jnp.logical_and(gap >= half - 1, gap <= half + 1)

    n_direct = sum(direct(t).astype(jnp.int32) for t in range(low_groups))

    def greet_ctx(i):
        @pl.when(2 * i != s)
        def _():
            greet(h, 2 * i)

    def alike(j):
        return lax.rem(h + GROUP * j, heads)

    def far_first(act):
        for i in range(groups // 2):
            act(alike(groups // 2 - i))
            if i > 0:
                act(alike(groups // 2 + i))

    mate_kind = {0: kind, 1: kind + 1 - 2 * lax.rem(kind, 2), 2: lax.rem(kind + 2, GROUP), 3: GROUP - 1 - kind}

    def mate(d):
        return h - kind + mate_kind[d]

    loop(0, shards // 2, greet_ctx)
    for load in loads:
        load.start()
    far_first(lambda q: greet(q, my_desk))
    for d in range(1, GROUP):
        greet(mate(d), s - core)

    @pl.when(low)
    def _():
        for j in (half, half + 1, half - 1):
            for d in range(1, GROUP):
                greet(lax.rem(mate(d) + GROUP * j, heads), my_desk)
            g_far[lax.rem(group + j, groups)] = jnp.zeros((owned, width), BF16)

    @pl.when(jnp.logical_not(low))
    def _():
        g_dir[...] = jnp.zeros_like(g_dir)

    loads[0].wait()
    loads[1].wait()
    raw = lat_ref[...].astype(F32)
    rms = lax.rsqrt(jnp.mean(raw * raw, axis=1, keepdims=True) + 1e-06)
    hat = raw * rms
    gain = gain_ref[...]
    own_n[...] = (hat * gain).astype(BF16)
    n_buf[group] = own_n[...]

    def peer(dx, dy, dc):
        x, y = lax.rem(s // 4 + dx, 4), lax.rem(s // 2 + dy, 2)
        return 4 * x + 2 * y + lax.rem(core + dc, 2)

    def tell(t, go):
        pl.semaphore_signal(
            go, 1, device_id={"head": h, "ctx": t}, device_id_type=MESH
        )

    def gate(desk, expected, listeners, go):
        @pl.when(s == desk)
        def _():
            pl.semaphore_wait(barrier, expected)
            for t in listeners:
                if t is partner:
                    tell(t, go)
                else:
                    pl.when(t != desk)(functools.partial(tell, t, go))

        @pl.when(s != desk)
        def _():
            pl.semaphore_wait(go, 1)

    def send(axis, q, src, dst, lane):
        pltpu.make_async_remote_copy(
            src_ref=src,
            dst_ref=dst,
            send_sem=send_sems.at[lane],
            recv_sem=recv_sems.at[lane],
            device_id={axis: q},
            device_id_type=MESH,
        ).start()

    with jax.named_scope("gate_ctx"):
        gate(s - core, shards - 1 + 2 * (GROUP - 1), (partner,), ctx_go)
    loads[3].wait()

    def send_ctx(i, src, dst, lane):
        q = lax.rem(s + i, shards)
        send("ctx", q, src(q), dst, lane)

    for turn in TURNS:
        send("ctx", peer(*turn), w_buf.at[s], w_buf.at[s], 0)

    def to_low(act):
        far_first(lambda q: pl.when(q < SPLIT)(lambda: act(q)))

    def to_high(act):
        far_first(lambda q: pl.when(q >= SPLIT)(lambda: act(q)))

    def send_n(q):
        send("head", q, own_n, n_buf.at[group], 1)

    def send_far(q):
        send("head", q, far_send.at[q // GROUP], g_far.at[group], 2)

    def send_cot():
        loop(1, shards, lambda i: send_ctx(i, lambda q: cot_all.at[s], cot_all.at[s], 5))

    mine = low.astype(jnp.int32)

    def low_rows():
        with jax.named_scope("gate_low"):
            expected = 4 * (low_groups - mine + (GROUP - 1) * n_direct)
            gate(desks[0], expected, cell_members, low_go)
        to_low(send_n)

    pl.when(jnp.logical_not(low))(low_rows)

    loads[2].wait()
    cot_mat = cot_all.at[s]
    for p in range(heads):
        at = p // GROUP * owned
        row = (at // SUB * GROUP + p % GROUP) * SUB + at % SUB
        cot_mat[row : row + owned, :] = cot_ref[owned * p : owned * (p + 1), :]

    pl.when(low)(send_cot)

    with jax.named_scope("wait_w"):
        drain(w_buf.at[pl.ds(0, shards - 1)], recv_sems.at[0])
    whole = w_buf[...].reshape(width, -1)
    g = lax.dot_general(
        cot_mat[...], whole, (((1,), (1,)), ((), ())), preferred_element_type=F32
    )
    for k in range(GROUP):
        starts = [(b * GROUP + k) * SUB for b in range(blocks)]
        g_k = jnp.concatenate([g[r : r + SUB, :] for r in starts], axis=0)
        g_mat[k] = g_k
        g_send[k] = g_k.astype(BF16)
    for d in (3, 1, 2):
        send("head", mate(d), g_send.at[mate_kind[d]], g_near.at[d - 1], 3)
    for t in range(low_groups):
        for k in range(GROUP):
            r = (owned * t // SUB * GROUP + k) * SUB + owned * t % SUB
            dir_send[GROUP * t + k] = g[r : r + owned, :].astype(BF16)
        slot = (lax.rem(group - t + groups, groups) - half + 1) * GROUP + kind

        @pl.when(direct(t))
        def _():
            for k in range(GROUP):
                q = GROUP * t + k
                send("head", q, dir_send.at[q], g_dir.at[slot], 6)

    pl.when(low)(low_rows)

    with jax.named_scope("wait_near"):
        drain(g_near, recv_sems.at[3])
    part = g_mat[kind] + jnp.sum(g_near[...].astype(F32), axis=0)
    part = part.astype(BF16)
    for j in range(groups):
        far_send[j] = part[owned * j : owned * (j + 1), :]
    g_far[group] = far_send[group]

    to_low(lambda q: pl.when(jnp.logical_not(direct(q // GROUP)))(lambda: send_far(q)))
    with jax.named_scope("gate_high"):
        gate(desks[1], 4 * (groups - low_groups - 1 + mine), cell_members, high_go)
    to_high(send_n)
    to_high(send_far)
    pl.when(jnp.logical_not(low))(send_cot)

    with jax.named_scope("wait_n1"):
        drain(n_buf.at[pl.ds(0, groups - 1)], recv_sems.at[1])
    rows = jnp.concatenate([n_buf[j].astype(F32) for j in range(groups)], axis=0)
    strip = width // shards
    lanes = strip * blocks
    lane_block = lax.broadcasted_iota(jnp.int32, (SUB, lanes), 1) // strip
    for q in range(shards):
        base, turn = q * strip // lanes * lanes, q * strip % lanes
        packed = None
        for b in range(blocks):
            tile = rows[b * SUB : (b + 1) * SUB, base : base + lanes]
            shift = (b * strip - turn) % lanes
            tile = pltpu.roll(tile, shift, 1) if shift else tile
            packed = tile if b == 0 else jnp.where(lane_block == b, tile, packed)
        pk_send[q] = packed.astype(BF16)
    slot = s * GROUP + kind
    pk_recv[slot] = pk_send[s]

    for dx, dy, dc in TURNS + ((0, 0, 0),):
        q = peer(dx, dy, dc)
        for d in (3, 1, 2, 0):
            if dx or dy or dc or d:
                pltpu.make_async_remote_copy(
                    src_ref=pk_send.at[q],
                    dst_ref=pk_recv.at[slot],
                    send_sem=send_sems.at[4],
                    recv_sem=recv_sems.at[4],
                    device_id={"head": mate(d), "ctx": q},
                    device_id_type=MESH,
                ).start()

    with jax.named_scope("wait_g"):

        @pl.when(low)
        def _():
            drain(g_far.at[pl.ds(0, groups - 4)], recv_sems.at[2])
            drain(g_dir, recv_sems.at[6])

        @pl.when(jnp.logical_not(low))
        def _():
            drain(g_far.at[pl.ds(0, groups - 1)], recv_sems.at[2])

    total = jnp.sum(g_far[...].astype(F32), axis=0) + jnp.sum(g_dir[...].astype(F32), axis=0)
    scaled = total * gain
    inner = jnp.mean(scaled * hat, axis=1, keepdims=True)
    lg_ref[...] = rms * (scaled - hat * inner)

    with jax.named_scope("wait_cot"):
        drain(cot_all.at[pl.ds(0, shards - 1)], recv_sems.at[5])
    with jax.named_scope("wait_pk"):
        drain(pk_recv.at[pl.ds(0, GROUP * shards - 1)], recv_sems.at[4])
    strips = pk_recv[...].astype(F32).reshape(-1, lanes).T.astype(BF16)
    wg = jnp.zeros((strip, w_buf.shape[2]), F32)
    for b in range(blocks):
        cot_b = cot_all[:, b * GROUP * SUB : (b + 1) * GROUP * SUB, :]
        wg = wg + lax.dot_general(
            strips[b * strip : (b + 1) * strip, :],
            cot_b.reshape(-1, cot_b.shape[2]),
            (((1,), (0,)), ((), ())),
            preferred_element_type=F32,
        )
    wg_ref[...] = wg.reshape(wg_ref.shape)

    with jax.named_scope("drain"):
        drain(w_buf.at[pl.ds(0, shards - 1)], send_sems.at[0])
        drain(n_buf.at[pl.ds(0, groups - 1)], send_sems.at[1])
        for n in range(4):

            @pl.when(n_direct == n)
            def _():
                drain(g_far.at[pl.ds(0, groups - 1 - n)], send_sems.at[2])
                if n:
                    drain(g_dir.at[pl.ds(0, GROUP * n)], send_sems.at[6])

        drain(g_near, send_sems.at[3])
        drain(pk_recv.at[pl.ds(0, GROUP * shards - 1)], send_sems.at[4])
        drain(cot_all.at[pl.ds(0, shards - 1)], send_sems.at[5])


def put(lg_ref, wg_ref, lg_out, wg_out, sems):
    lg = pltpu.make_async_copy(lg_ref, lg_out, sems.at[0])
    wg = pltpu.make_async_copy(wg_ref, wg_out, sems.at[1])
    wg.start()
    lg.start()
    lg.wait()
    wg.wait()


def solution(mesh):
    heads, shards = mesh.shape["head"], mesh.shape["ctx"]

    def per_device(latent, gain, cotangent, weight):
        _, owned, width = latent.shape
        tokens, channels = cotangent.shape[1], cotangent.shape[3]
        rows = weight.shape[0]
        groups = heads // GROUP
        span = groups * owned
        vmem = pl.BlockSpec(memory_space=pltpu.VMEM)
        lg, wg = pl.pallas_call(
            functools.partial(kernel, heads, shards),
            out_shape=(
                pltpu.VMEM((owned, width), F32),
                pltpu.VMEM((rows, 1, channels), F32),
            ),
            in_specs=[pl.BlockSpec(memory_space=pl.ANY)] * 4,
            out_specs=(vmem, vmem),
            scratch_shapes=[
                pltpu.VMEM((owned, width), BF16),
                pltpu.VMEM((1, width), F32),
                pltpu.VMEM((tokens, channels), BF16),
                pltpu.VMEM((shards, tokens, channels), BF16),
                pltpu.VMEM((owned, width), BF16),
                pltpu.VMEM((groups, owned, width), BF16),
                pltpu.VMEM((shards, rows, channels), BF16),
                pltpu.VMEM((GROUP, span, width), F32),
                pltpu.VMEM((GROUP, span, width), BF16),
                pltpu.VMEM((GROUP - 1, span, width), BF16),
                pltpu.VMEM((groups, owned, width), BF16),
                pltpu.VMEM((groups, owned, width), BF16),
                pltpu.VMEM((SPLIT, owned, width), BF16),
                pltpu.VMEM((3 * GROUP, owned, width), BF16),
                pltpu.VMEM((shards, SUB, width // shards * span // SUB), BF16),
                pltpu.VMEM((GROUP * shards, SUB, width // shards * span // SUB), BF16),
                pltpu.SemaphoreType.DMA((4,)),
                pltpu.SemaphoreType.DMA((7,)),
                pltpu.SemaphoreType.DMA((7,)),
                pltpu.SemaphoreType.REGULAR,
                pltpu.SemaphoreType.REGULAR,
                pltpu.SemaphoreType.REGULAR,
            ],
            compiler_params=pltpu.CompilerParams(collective_id=0, has_side_effects=True),
            name="fused",
        )(
            latent.reshape(owned, width),
            gain.reshape(1, width),
            cotangent.reshape(tokens, channels),
            weight.reshape(rows, channels),
        )
        lg, wg = pl.pallas_call(
            put,
            out_shape=(
                jax.ShapeDtypeStruct((owned, width), F32),
                jax.ShapeDtypeStruct((rows, 1, channels), F32),
            ),
            in_specs=[vmem, vmem],
            out_specs=(pl.BlockSpec(memory_space=pl.ANY), pl.BlockSpec(memory_space=pl.ANY)),
            scratch_shapes=[pltpu.SemaphoreType.DMA((2,))],
            name="put",
        )(
            pltpu.with_memory_space_constraint(lg, pltpu.VMEM),
            pltpu.with_memory_space_constraint(wg, pltpu.VMEM),
        )
        return lg.reshape(latent.shape), wg.reshape(weight.shape)

    return jax.shard_map(
        per_device,
        mesh=mesh,
        in_specs=(
            P("ctx", "head", None),
            P(),
            P("ctx", None, "head", None),
            P("ctx", "head", None),
        ),
        out_specs=(P("ctx", "head", None), P("ctx", "head", None)),
        check_vma=False,
    )
```
